1024 devices in a mesh: section: 4 (over y), hid: 32 (over z), wid: 8 (over x, core).
Axes of the slice: x: 4, y: 4, z: 32, core: 2. Of those that a mesh axis runs over, the one named last changes fastest.
Arguments:
- out_grad: bfloat16 [512, 8192], P(('section', 'hid'), 'wid'), may hold values from -6 to 6
- inputs: bfloat16 [512, 8192], P(('section', 'hid'), 'wid'), may hold values from -6 to 6
- gate_pre: bfloat16 [512, 14336], P(('section', 'wid'), 'hid'), may hold values from -6 to 6
- up_pre: bfloat16 [512, 14336], P(('section', 'wid'), 'hid'), may hold values from -6 to 6
- w1_values: bfloat16 [40960, 4096], P(('section', 'hid', 'wid')), may hold values from -0.09375 to 0.09375
- w1_index: int32 [40960], P(('section', 'hid', 'wid')), may hold values from 0 to 112, as said below
- w3_values: bfloat16 [40960, 4096], P(('section', 'hid', 'wid')), may hold values from -0.09375 to 0.09375
- w3_index: int32 [40960], P(('section', 'hid', 'wid')), may hold values from 0 to 112, as said below
- w2_values: bfloat16 [40960, 4096], P(('section', 'hid', 'wid')), may hold values from -0.125 to 0.125
- w2_index: int32 [40960], P(('section', 'hid', 'wid')), may hold values from 0 to 112, as said below
Outputs:
- input_grad: bfloat16 [512, 8192], P(('section', 'hid'), 'wid')
- w1_grad: bfloat16 [40960, 4096], P(('section', 'hid', 'wid'))
- w3_grad: bfloat16 [40960, 4096], P(('section', 'hid', 'wid'))
- w2_grad: bfloat16 [40960, 4096], P(('section', 'hid', 'wid'))
The draws below stay inside these ranges and needn't reach their ends.
Inputs may be any that keep to these rules, and one draw needn't show every extreme that they name: `w1_index`: on each device, its 40 slots hold distinct block numbers of its tile first, then the tile's block count in every unused slot; the number of used slots differs from device to device, and some device of every matrix uses all 40. `w3_index`: as for w1_index. `w2_index`: as for w1_index.
All inputs are finite; a program needn't handle non-finite values.
Results may differ from the reference program's by a relative error of at most 0.0049.
Values may be sent and summed in bfloat16 or wider, within the bound.
No kernel may reach another device: no remote copies, remote signals or barrier semaphores. Data moves between devices by JAX's collectives and lax.ppermute only.
A program may use at most 32 MiB of HBM per device.

```python
import jax
import jax.numpy as jnp
from jax import lax

D = 8192
FF = 14336
BLOCK = 64
CAP = 40
TOK = 128
TOKENS = 512
SLOTS = 40960
N_SECTION = 4
N_HID = 32
N_WID = 8


def slot_blocks(key, salt):
    local_blocks = D // N_WID // BLOCK * (FF // N_HID // BLOCK)
    devices = SLOTS // CAP
    base = jax.random.fold_in(key, salt)
    keys = jax.random.split(jax.random.fold_in(base, 1), devices)
    orders = jax.vmap(lambda k: jax.random.permutation(k, local_blocks))(keys)
    counts = jax.random.randint(jax.random.fold_in(base, 2), (devices,), CAP // 8, CAP + 1)
    fullest = jax.random.randint(jax.random.fold_in(base, 3), (), 0, devices)
    counts = jnp.where(jnp.arange(devices) == fullest, CAP, counts)
    slot = jnp.arange(CAP)
    index = jnp.where(slot[None, :] < counts[:, None], orders[:, :CAP], local_blocks)
    return index.reshape(-1).astype(jnp.int32)


def draw_w1_index(key, part):
    return slot_blocks(key, 101)


def draw_w3_index(key, part):
    return slot_blocks(key, 203)


def draw_w2_index(key, part):
    return slot_blocks(key, 307)


def shard_levels(key, dims, cuts, least, high):
    def one(position, blocks):
        draws = jax.random.uniform(jax.random.fold_in(jax.random.fold_in(key, 6), position), (blocks,), jnp.float32, least / len(cuts), high / len(cuts))
        return jnp.repeat(jnp.exp(draws), dims[position] // blocks).reshape((-1,) + (1,) * (len(dims) - position - 1))

    level = one(*cuts[0])
    for cut in cuts[1:]:
        level = level * one(*cut)
    return level


def bell_draw(key, shape, scale, most, cuts=(), kind=jnp.bfloat16):
    level = shard_levels(key, shape, cuts, -0.22, 0.18) if cuts else 1.0
    entries = jax.random.normal(key, shape, jnp.float32) * scale * level
    return jnp.minimum(jnp.maximum(entries, -most), most).astype(kind)


def setup_inputs(seed: int = 0) -> dict:
    seeds = jax.random.split(jax.random.key(seed), 11)
    out_grad = bell_draw(seeds[0], (TOKENS, D), 1.0, 6.0, ((0, 128), (1, 8)))
    inputs = bell_draw(seeds[1], (TOKENS, D), 1.0, 6.0, ((0, 128), (1, 8)))
    gate_pre = bell_draw(seeds[2], (TOKENS, FF), 1.5, 6.0, ((0, 32), (1, 32)))
    up_pre = bell_draw(seeds[3], (TOKENS, FF), 1.0, 6.0, ((0, 32), (1, 32)))
    w1_values = bell_draw(seeds[4], (SLOTS, BLOCK * BLOCK), (FF // 4) ** -0.5, 0.09375, ((0, 1024),))
    w1_index = draw_w1_index(jax.random.fold_in(seeds[10], 71), 0)
    w3_values = bell_draw(seeds[6], (SLOTS, BLOCK * BLOCK), (FF // 4) ** -0.5, 0.09375, ((0, 1024),))
    w3_index = draw_w3_index(jax.random.fold_in(seeds[10], 71), 0)
    w2_values = bell_draw(seeds[8], (SLOTS, BLOCK * BLOCK), (D // 4) ** -0.5, 0.125, ((0, 1024),))
    w2_index = draw_w2_index(jax.random.fold_in(seeds[10], 71), 0)
    return {"out_grad": out_grad, "inputs": inputs, "gate_pre": gate_pre, "up_pre": up_pre, "w1_values": w1_values, "w1_index": w1_index, "w3_values": w3_values, "w3_index": w3_index, "w2_values": w2_values, "w2_index": w2_index}


def dense_local(values, index, rows, cols):
    blocks = values.reshape(values.shape[0], BLOCK, BLOCK)
    total = rows * cols
    holder = jnp.zeros((total + 1, BLOCK, BLOCK), values.dtype).at[index].set(blocks)
    return holder[:total].reshape(rows, cols, BLOCK, BLOCK).transpose(0, 2, 1, 3).reshape(rows * BLOCK, cols * BLOCK)


def slots_from(dense, index, rows, cols):
    blocks = dense.reshape(rows, BLOCK, cols, BLOCK).transpose(0, 2, 1, 3).reshape(rows * cols, BLOCK, BLOCK)
    blocks = jnp.concatenate([blocks, jnp.zeros((1, BLOCK, BLOCK), dense.dtype)], axis=0)
    return blocks[index].reshape(index.shape[0], BLOCK * BLOCK)


def swiglu_grads(hidden_grad, gate_pre, up_pre):
    gate = gate_pre.astype(jnp.float32)
    upval = up_pre.astype(jnp.float32)
    sigma = jax.nn.sigmoid(gate)
    gate_grad = (hidden_grad * upval * sigma * (1.0 + gate * (1.0 - sigma))).astype(jnp.bfloat16)
    up_grad = (hidden_grad * gate * sigma).astype(jnp.bfloat16)
    activ = (gate * sigma * upval).astype(jnp.bfloat16)
    return gate_grad, up_grad, activ


def fdot(left, right):
    return jnp.dot(left.astype(jnp.float32), right.astype(jnp.float32), precision=lax.Precision.HIGHEST)


def reference(out_grad, inputs, gate_pre, up_pre, w1_values, w1_index, w3_values, w3_index, w2_values, w2_index):
    rows = D // N_WID // BLOCK
    cols = FF // N_HID // BLOCK
    tile_d = D // N_WID
    tile_f = FF // N_HID
    input_list, first_list, third_list, second_list = [], [], [], []
    for section in range(N_SECTION):
        after = (section + 1) % N_SECTION
        grad_rows = out_grad[after * TOK:(after + 1) * TOK]
        xrows = inputs[section * TOK:(section + 1) * TOK]
        gate = gate_pre[section * TOK:(section + 1) * TOK]
        upval = up_pre[section * TOK:(section + 1) * TOK]

        def build(values, index, r, c):
            vals = values.reshape(N_SECTION, N_HID, N_WID, CAP, BLOCK * BLOCK)[section]
            idx = index.reshape(N_SECTION, N_HID, N_WID, CAP)[section]
            local = jax.vmap(jax.vmap(lambda v, i: dense_local(v, i, r, c)))(vals, idx)
            return local, idx

        loc1, idx1 = build(w1_values, w1_index, rows, cols)
        loc3, idx3 = build(w3_values, w3_index, rows, cols)
        loc2, idx2 = build(w2_values, w2_index, cols, rows)
        first = loc1.transpose(1, 2, 0, 3).reshape(D, FF)
        third = loc3.transpose(1, 2, 0, 3).reshape(D, FF)
        second = loc2.transpose(0, 2, 1, 3).reshape(FF, D)
        hidden_grad = fdot(grad_rows, second.T)
        gate_grad, up_grad, activ = swiglu_grads(hidden_grad, gate, upval)
        input_list.append((fdot(gate_grad, first.T) + fdot(up_grad, third.T)).astype(jnp.bfloat16))
        g1 = fdot(xrows.T, gate_grad).astype(jnp.bfloat16)
        g3 = fdot(xrows.T, up_grad).astype(jnp.bfloat16)
        g2 = fdot(activ.T, grad_rows).astype(jnp.bfloat16)
        g1 = g1.reshape(N_WID, tile_d, N_HID, tile_f).transpose(2, 0, 1, 3)
        g3 = g3.reshape(N_WID, tile_d, N_HID, tile_f).transpose(2, 0, 1, 3)
        g2 = g2.reshape(N_HID, tile_f, N_WID, tile_d).transpose(0, 2, 1, 3)
        pick_wide = jax.vmap(jax.vmap(lambda m, i: slots_from(m, i, rows, cols)))
        pick_tall = jax.vmap(jax.vmap(lambda m, i: slots_from(m, i, cols, rows)))
        first_list.append(pick_wide(g1, idx1))
        third_list.append(pick_wide(g3, idx3))
        second_list.append(pick_tall(g2, idx2))
    input_grad = jnp.concatenate(input_list, axis=0)
    w1_grad = jnp.stack(first_list).reshape(SLOTS, BLOCK * BLOCK)
    w3_grad = jnp.stack(third_list).reshape(SLOTS, BLOCK * BLOCK)
    w2_grad = jnp.stack(second_list).reshape(SLOTS, BLOCK * BLOCK)
    return (input_grad, w1_grad, w3_grad, w2_grad)
```

```python
import functools

import jax
import jax.numpy as jnp
from jax import lax
from jax.experimental import pallas as pl
from jax.experimental.pallas import tpu as pltpu
from jax.sharding import PartitionSpec as P

BLOCK = 64
F32, BF16 = jnp.float32, jnp.bfloat16
NT = (((1,), (1,)), ((), ()))
TN = (((0,), (0,)), ((), ()))


def left_half(shape):
    return lax.broadcasted_iota(jnp.int32, shape, len(shape) - 1) < BLOCK


def unpack_blocks(values, spread, cap):
    mask = left_half((cap, 128))
    for pair in range(BLOCK // 2):
        rows = values[:, 128 * pair : 128 * pair + 128].astype(F32)
        turned = pltpu.roll(rows, BLOCK, 1)
        spread[pl.ds(2 * pair, cap, stride=BLOCK), :] = jnp.where(mask, rows, turned)
        spread[pl.ds(2 * pair + 1, cap, stride=BLOCK), :] = jnp.where(mask, turned, rows)


def place_blocks(index, spread, dense, cols, cap):
    lane = lax.broadcasted_iota(jnp.int32, (BLOCK, 128), 1) // BLOCK

    def step(slot, carry):
        number = index[slot]
        row = number // cols
        col = number - row * cols
        block = spread[pl.ds(pl.multiple_of(slot * BLOCK, BLOCK), BLOCK), :].astype(BF16)
        down = pl.ds(pl.multiple_of(row * BLOCK, BLOCK), BLOCK)
        along = pl.ds(pl.multiple_of(col // 2 * 128, 128), 128)
        old = dense[down, along]
        dense[down, along] = jnp.where(lane == col % 2, block, old)
        return carry

    lax.fori_loop(0, cap, step, 0, unroll=4)


def dense_kernel(index, values, dense, spread, *, cols):
    cap = values.shape[0]
    dense[...] = jnp.zeros_like(dense)
    unpack_blocks(values, spread, cap)
    place_blocks(index, spread, dense, cols, cap)


def take_blocks(index, dense, picked, cols, cap):
    def step(slot, carry):
        number = index[slot]
        row = number // cols
        col = number - row * cols
        down = pl.ds(pl.multiple_of(row * BLOCK, BLOCK), BLOCK)
        along = pl.ds(pl.multiple_of(col // 2 * 128, 128), 128)
        block = pltpu.roll(dense[down, along], col % 2 * BLOCK, 1)
        picked[pl.ds(pl.multiple_of(slot * BLOCK, BLOCK), BLOCK), :] = block
        return carry

    lax.fori_loop(0, cap, step, 0, unroll=4)


def pack_blocks(picked, out, cap):
    mask = left_half((cap, 128))
    for pair in range(BLOCK // 2):
        upper = picked[pl.ds(2 * pair, cap, stride=BLOCK), :]
        lower = pltpu.roll(picked[pl.ds(2 * pair + 1, cap, stride=BLOCK), :], BLOCK, 1)
        out[:, 128 * pair : 128 * pair + 128] = jnp.where(mask, upper, lower).astype(BF16)


def hidden_kernel(tokens, dense, out):
    prod = lax.dot_general(tokens[...], dense[...], NT, preferred_element_type=F32)
    width = prod.shape[1]
    top = lax.broadcasted_iota(jnp.int32, (8, width), 0) < 4
    half = prod.shape[0] // 2
    for k in range(half // 8):
        even = prod[8 * k : 8 * k + 8]
        odd = prod[half + 8 * k : half + 8 * k + 8]
        out[8 * k : 8 * k + 8, :] = jnp.where(top, even, pltpu.roll(odd, 4, 0))


def gate_kernel(parts, gate, up, out):
    width = gate.shape[1]
    total = parts[0]
    for i in range(1, parts.shape[0]):
        total = total + parts[i]
    hidden = total[:, :width]
    g = gate[...].astype(F32)
    u = up[...].astype(F32)
    sigma = 1.0 / (1.0 + jnp.exp(-g))
    gate_grad = (hidden * u * sigma * (1.0 + g * (1.0 - sigma))).astype(BF16)
    up_grad = (hidden * g * sigma).astype(BF16)
    activ = (g * sigma * u).astype(BF16)
    out[...] = jnp.zeros_like(out)
    for peer in range(out.shape[0]):
        out[peer, 0, :, :width] = gate_grad
        out[peer, 1, :, :width] = up_grad
        out[peer, 2, :, :width] = activ


def all_rows(acts, which):
    picked = acts[:, which]
    return picked.reshape(picked.shape[0] * picked.shape[1], picked.shape[2])


def input_kernel(acts, d1, d3, out):
    half = out.shape[1]
    rows = 2 * half
    prod = lax.dot_general(all_rows(acts, 0), d1[:rows], NT, preferred_element_type=F32)
    prod = prod + lax.dot_general(all_rows(acts, 1), d3[:rows], NT, preferred_element_type=F32)
    top = lax.broadcasted_iota(jnp.int32, (8, half), 0) < 4
    across = out.shape[0] // 32

    def folded(peer):
        tile = prod[8 * (peer // 2) : 8 * (peer // 2) + 8]
        left, right = tile[:, :half], tile[:, half:]
        if peer % 2:
            return jnp.where(top, pltpu.roll(left, 4, 0), right)
        return jnp.where(top, left, pltpu.roll(right, 4, 0))

    for q in range(4):
        for b in range(0, across, 2):
            base = (q * across + b) * 8
            both = [folded(4 * b + q), folded(4 * b + 4 + q)]
            out[base : base + 16, :] = jnp.concatenate(both, 0).astype(BF16)


def near_kernel(parts, out):
    total = parts[0].astype(F32)
    for i in range(1, parts.shape[0]):
        total = total + parts[i].astype(F32)
    out[...] = total.astype(BF16)


def far_kernel(parts, out):
    total = parts[0].astype(F32)
    for i in range(1, parts.shape[0]):
        total = total + parts[i].astype(F32)
    half = total.shape[1]
    out[:, :half] = total[:4].astype(BF16)
    out[:, half:] = pltpu.roll(total, 4, 0)[:4].astype(BF16)


def weight_kernel(i1, i3, i2, tokens, acts, o1, o3, o2, spaced, dense, tall, picked, *, rows, cols):
    cap = o1.shape[0]
    count, width = acts.shape[0] * acts.shape[2], acts.shape[3]
    top = lax.broadcasted_iota(jnp.int32, (8, width), 0) < 4
    zero = jnp.zeros((8, width), F32)

    def spread_rows(which, upper):
        full = all_rows(acts, which).astype(F32)
        for k in range(count // 8):
            piece = full[8 * k : 8 * k + 8]
            turned = pltpu.roll(piece, 4, 0)
            if upper:
                even, odd = jnp.where(top, piece, zero), jnp.where(top, turned, zero)
            else:
                even, odd = jnp.where(top, zero, turned), jnp.where(top, zero, piece)
            spaced[8 * k : 8 * k + 8, :] = even
            spaced[count + 8 * k : count + 8 * k + 8, :] = odd
        return spaced[...].astype(BF16)

    dense[rows * BLOCK :, :] = jnp.zeros((BLOCK, width), F32)
    for which, index, out in ((0, i1, o1), (1, i3, o3)):
        dense[: rows * BLOCK, :] = lax.dot_general(
            tokens[...], spread_rows(which, False), TN, preferred_element_type=F32)
        take_blocks(index, dense, picked, cols, cap)
        pack_blocks(picked, out, cap)
    tall[...] = lax.dot_general(spread_rows(2, True), tokens[...], TN, preferred_element_type=F32)
    take_blocks(i2, tall, picked, rows, cap)
    pack_blocks(picked, o2, cap)


def vm():
    return pl.BlockSpec(memory_space=pltpu.VMEM)


def sm():
    return pl.BlockSpec(memory_space=pltpu.SMEM)


def densify(index, values, rows, cols):
    cap = values.shape[0]
    wide = (cols + 1) // 2 * 128
    return pl.pallas_call(
        functools.partial(dense_kernel, cols=cols),
        out_shape=jax.ShapeDtypeStruct((rows * BLOCK + BLOCK, wide), BF16),
        in_specs=[sm(), vm()],
        out_specs=vm(),
        scratch_shapes=[pltpu.VMEM((cap * BLOCK, 128), F32)],
        name="densify",
    )(index, values)


def hidden(tokens, d2):
    return pl.pallas_call(hidden_kernel, out_shape=jax.ShapeDtypeStruct((tokens.shape[0] // 2, d2.shape[0]), F32),
        in_specs=[vm()] * 2, out_specs=vm(), name="hidden")(tokens, d2)


def gate(parts, g, u):
    return pl.pallas_call(gate_kernel, out_shape=jax.ShapeDtypeStruct((parts.shape[0], 3) + parts.shape[1:], BF16),
        in_specs=[vm()] * 3, out_specs=vm(), name="gate")(parts, g, u)


def inputg(acts, d1, d3, width):
    tokens = acts.shape[0] * acts.shape[2]
    return pl.pallas_call(
        input_kernel,
        out_shape=jax.ShapeDtypeStruct((2 * tokens, width // 2), BF16),
        in_specs=[vm()] * 3,
        out_specs=vm(),
        name="inputg",
    )(acts, d1, d3)


def near_sum(parts):
    return pl.pallas_call(
        near_kernel,
        out_shape=jax.ShapeDtypeStruct(parts.shape[1:], BF16),
        in_specs=[vm()],
        out_specs=vm(),
        name="near_sum",
    )(parts)


def far_sum(parts):
    return pl.pallas_call(
        far_kernel,
        out_shape=jax.ShapeDtypeStruct((parts.shape[1] // 2, 2 * parts.shape[2]), BF16),
        in_specs=[vm()],
        out_specs=vm(),
        name="far_sum",
    )(parts)


def weights(i1, i3, i2, tokens, acts, rows, cols):
    cap = i1.shape[0]
    wide = acts.shape[3]
    count = acts.shape[0] * acts.shape[2]
    o = jax.ShapeDtypeStruct((cap, BLOCK * BLOCK), BF16)
    return pl.pallas_call(
        functools.partial(weight_kernel, rows=rows, cols=cols), out_shape=(o, o, o),
        in_specs=[sm()] * 3 + [vm()] * 2, out_specs=(vm(),) * 3,
        scratch_shapes=[pltpu.VMEM((2 * count, wide), F32), pltpu.VMEM((rows * BLOCK + BLOCK, wide), F32),
            pltpu.VMEM((wide, rows * BLOCK), F32), pltpu.VMEM((cap * BLOCK, 128), F32)],
        name="weights")(i1, i3, i2, tokens, acts)


def strided(peers, by):
    return [list(range(first, peers, by)) for first in range(by)]


def adjacent(peers, many):
    return [list(range(first, first + many)) for first in range(0, peers, many)]


def gather_tokens(both):
    peers = lax.axis_size("hid")
    skipping = lax.all_gather(both, "hid", axis=0, tiled=True, axis_index_groups=strided(peers, 2))
    return lax.all_gather(skipping, "hid", axis=0, tiled=True, axis_index_groups=adjacent(peers, 2))


def exchange(chunks, groups):
    return lax.all_to_all(chunks, "hid", 0, 0, tiled=True, axis_index_groups=groups)


def scatter_sum(total):
    peers = lax.axis_size("hid")
    width = total.shape[1]
    near = near_sum(exchange(total.reshape(4, -1, width), adjacent(peers, 4)))
    return far_sum(exchange(near.reshape(peers // 4, -1, width), strided(peers, 4)))


def body(
    out_grad,
    inputs,
    gate_pre,
    up_pre,
    w1_values,
    w1_index,
    w3_values,
    w3_index,
    w2_values,
    w2_index,
):
    rows = inputs.shape[1] // BLOCK
    cols = gate_pre.shape[1] // BLOCK
    sections = lax.axis_size("section")
    arrived = lax.ppermute(out_grad, "section", [(i, (i - 1) % sections) for i in range(sections)])
    tokens = gather_tokens(jnp.concatenate([arrived, inputs], axis=0))
    second = densify(w2_index, w2_values, cols, rows)
    first = densify(w1_index, w1_values, rows, cols)
    third = densify(w3_index, w3_values, rows, cols)
    partial_grad = hidden(tokens, second)
    peers = lax.axis_size("wid")
    parts = partial_grad.reshape(peers, partial_grad.shape[0] // peers, partial_grad.shape[1])
    parts = lax.all_to_all(parts, "wid", 0, 0, tiled=True)
    acts = lax.all_to_all(gate(parts, gate_pre, up_pre), "wid", 0, 0, tiled=True)
    input_grad = scatter_sum(inputg(acts, first, third, inputs.shape[1]))
    w1_grad, w3_grad, w2_grad = weights(w1_index, w3_index, w2_index, tokens, acts, rows, cols)
    return (input_grad, w1_grad, w3_grad, w2_grad)


def solution(mesh):
    in_specs = (
        P(("section", "hid"), "wid"),
        P(("section", "hid"), "wid"),
        P(("section", "wid"), "hid"),
        P(("section", "wid"), "hid"),
        P(("section", "hid", "wid"), None),
        P(("section", "hid", "wid")),
        P(("section", "hid", "wid"), None),
        P(("section", "hid", "wid")),
        P(("section", "hid", "wid"), None),
        P(("section", "hid", "wid")),
    )
    out_specs = (
        P(("section", "hid"), "wid"),
        P(("section", "hid", "wid"), None),
        P(("section", "hid", "wid"), None),
        P(("section", "hid", "wid"), None),
    )
    return jax.shard_map(body, mesh=mesh, in_specs=in_specs, out_specs=out_specs, check_vma=False)
```

```python
import functools

import jax
import jax.numpy as jnp
from jax import lax
from jax.experimental import pallas as pl
from jax.experimental.pallas import tpu as pltpu
from jax.sharding import PartitionSpec as P

BLOCK = 64
GRANT = 16 << 20
F32, BF16 = jnp.float32, jnp.bfloat16
NT = (((1,), (1,)), ((), ()))
TN = (((0,), (0,)), ((), ()))


def left_half(shape):
    return lax.broadcasted_iota(jnp.int32, shape, len(shape) - 1) < BLOCK


def unpack_blocks(values, spread, cap):
    mask = left_half((cap, 128))
    for pair in range(BLOCK // 2):
        rows = values[:, 128 * pair : 128 * pair + 128].astype(F32)
        turned = pltpu.roll(rows, BLOCK, 1)
        spread[pl.ds(2 * pair, cap, stride=BLOCK), :] = jnp.where(mask, rows, turned)
        spread[pl.ds(2 * pair + 1, cap, stride=BLOCK), :] = jnp.where(mask, turned, rows)


def place_blocks(index, spread, dense, cols, cap):
    lane = lax.broadcasted_iota(jnp.int32, (BLOCK, 128), 1) // BLOCK

    def step(slot, carry):
        number = index[slot]
        row = number // cols
        col = number - row * cols
        block = spread[pl.ds(pl.multiple_of(slot * BLOCK, BLOCK), BLOCK), :].astype(BF16)
        down = pl.ds(pl.multiple_of(row * BLOCK, BLOCK), BLOCK)
        along = pl.ds(pl.multiple_of(col // 2 * 128, 128), 128)
        old = dense[down, along]
        dense[down, along] = jnp.where(lane == col % 2, block, old)
        return carry

    lax.fori_loop(0, cap, step, 0, unroll=4)


def dense_kernel(index, values, dense, spread, *, cols):
    cap = values.shape[0]
    dense[...] = jnp.zeros_like(dense)
    unpack_blocks(values, spread, cap)
    place_blocks(index, spread, dense, cols, cap)


def take_blocks(index, dense, picked, cols, cap):
    def step(slot, carry):
        number = index[slot]
        row = number // cols
        col = number - row * cols
        down = pl.ds(pl.multiple_of(row * BLOCK, BLOCK), BLOCK)
        along = pl.ds(pl.multiple_of(col // 2 * 128, 128), 128)
        block = pltpu.roll(dense[down, along], col % 2 * BLOCK, 1)
        picked[pl.ds(pl.multiple_of(slot * BLOCK, BLOCK), BLOCK), :] = block
        return carry

    lax.fori_loop(0, cap, step, 0, unroll=4)


def pack_blocks(picked, out, cap):
    mask = left_half((cap, 128))
    for pair in range(BLOCK // 2):
        upper = picked[pl.ds(2 * pair, cap, stride=BLOCK), :]
        lower = pltpu.roll(picked[pl.ds(2 * pair + 1, cap, stride=BLOCK), :], BLOCK, 1)
        out[:, 128 * pair : 128 * pair + 128] = jnp.where(mask, upper, lower).astype(BF16)


def hidden_kernel(tokens, dense, out):
    prod = lax.dot_general(tokens[...], dense[...], NT, preferred_element_type=F32)
    width = prod.shape[1]
    top = lax.broadcasted_iota(jnp.int32, (8, width), 0) < 4
    half = prod.shape[0] // 2
    for k in range(half // 8):
        even = prod[8 * k : 8 * k + 8]
        odd = prod[half + 8 * k : half + 8 * k + 8]
        out[8 * k : 8 * k + 8, :] = jnp.where(top, even, pltpu.roll(odd, 4, 0))


def gate_kernel(parts, gate, up, after, out):
    del after
    width = gate.shape[1]
    total = parts[0]
    for i in range(1, parts.shape[0]):
        total = total + parts[i]
    hidden = total[:, :width]
    g = gate[...].astype(F32)
    u = up[...].astype(F32)
    sigma = 1.0 / (1.0 + jnp.exp(-g))
    gate_grad = (hidden * u * sigma * (1.0 + g * (1.0 - sigma))).astype(BF16)
    up_grad = (hidden * g * sigma).astype(BF16)
    activ = (g * sigma * u).astype(BF16)
    out[...] = jnp.zeros_like(out)
    for peer in range(out.shape[0]):
        out[peer, 0, :, :width] = gate_grad
        out[peer, 1, :, :width] = up_grad
        out[peer, 2, :, :width] = activ


def all_rows(acts, which):
    picked = acts[:, which]
    return picked.reshape(picked.shape[0] * picked.shape[1], picked.shape[2])


def input_kernel(acts, d1, d3, out):
    half = out.shape[1]
    rows = 2 * half
    prod = lax.dot_general(all_rows(acts, 0), d1[:rows], NT, preferred_element_type=F32)
    prod = prod + lax.dot_general(all_rows(acts, 1), d3[:rows], NT, preferred_element_type=F32)
    top = lax.broadcasted_iota(jnp.int32, (8, half), 0) < 4
    across = out.shape[0] // 32

    def folded(peer):
        tile = prod[8 * (peer // 2) : 8 * (peer // 2) + 8]
        left, right = tile[:, :half], tile[:, half:]
        if peer % 2:
            return jnp.where(top, pltpu.roll(left, 4, 0), right)
        return jnp.where(top, left, pltpu.roll(right, 4, 0))

    for q in range(4):
        for b in range(0, across, 2):
            base = (q * across + b) * 8
            both = [folded(4 * b + q), folded(4 * b + 4 + q)]
            out[base : base + 16, :] = jnp.concatenate(both, 0).astype(BF16)


def near_kernel(parts, out):
    total = parts[0].astype(F32)
    for i in range(1, parts.shape[0]):
        total = total + parts[i].astype(F32)
    out[...] = total.astype(BF16)


def far_kernel(parts, out):
    total = parts[0].astype(F32)
    for i in range(1, parts.shape[0]):
        total = total + parts[i].astype(F32)
    half = total.shape[1]
    out[:, :half] = total[:4].astype(BF16)
    out[:, half:] = pltpu.roll(total, 4, 0)[:4].astype(BF16)


def weight_kernel(i1, i3, i2, tokens, acts, o1, o3, o2, spaced, dense, tall, picked, *, rows, cols):
    cap = o1.shape[0]
    count, width = acts.shape[0] * acts.shape[2], acts.shape[3]
    top = lax.broadcasted_iota(jnp.int32, (8, width), 0) < 4
    zero = jnp.zeros((8, width), F32)

    def spread_rows(which, upper):
        full = all_rows(acts, which).astype(F32)
        for k in range(count // 8):
            piece = full[8 * k : 8 * k + 8]
            turned = pltpu.roll(piece, 4, 0)
            if upper:
                even, odd = jnp.where(top, piece, zero), jnp.where(top, turned, zero)
            else:
                even, odd = jnp.where(top, zero, turned), jnp.where(top, zero, piece)
            spaced[8 * k : 8 * k + 8, :] = even
            spaced[count + 8 * k : count + 8 * k + 8, :] = odd
        return spaced[...].astype(BF16)

    dense[rows * BLOCK :, :] = jnp.zeros((BLOCK, width), F32)
    for which, index, out in ((0, i1, o1), (1, i3, o3)):
        dense[: rows * BLOCK, :] = lax.dot_general(
            tokens[...], spread_rows(which, False), TN, preferred_element_type=F32)
        take_blocks(index, dense, picked, cols, cap)
        pack_blocks(picked, out, cap)
    tall[...] = lax.dot_general(spread_rows(2, True), tokens[...], TN, preferred_element_type=F32)
    take_blocks(i2, tall, picked, rows, cap)
    pack_blocks(picked, o2, cap)


def vm():
    return pl.BlockSpec(memory_space=pltpu.VMEM)


def near(*arrays):
    return tuple(pltpu.with_memory_space_constraint(a, pltpu.VMEM) for a in arrays)


def on_chip(shape, dtype):
    return pltpu.VMEM(shape, dtype)


def sm():
    return pl.BlockSpec(memory_space=pltpu.SMEM)


def densify(index, values, rows, cols):
    cap = values.shape[0]
    wide = (cols + 1) // 2 * 128
    return pl.pallas_call(
        functools.partial(dense_kernel, cols=cols),
        out_shape=on_chip((rows * BLOCK + BLOCK, wide), BF16),
        in_specs=[sm(), vm()],
        out_specs=vm(),
        scratch_shapes=[pltpu.VMEM((cap * BLOCK, 128), F32)],
        compiler_params=pltpu.CompilerParams(vmem_limit_bytes=GRANT),
        name="densify",
    )(index, values)


def hidden(tokens, d2):
    return pl.pallas_call(
        hidden_kernel,
        out_shape=on_chip((tokens.shape[0] // 2, d2.shape[0]), F32),
        in_specs=[vm()] * 2,
        out_specs=vm(),
        compiler_params=pltpu.CompilerParams(vmem_limit_bytes=GRANT),
        name="hidden",
    )(*near(tokens, d2))


def gate(parts, gate_pre, up_pre, after):
    return pl.pallas_call(
        gate_kernel,
        out_shape=on_chip((parts.shape[0], 3) + parts.shape[1:], BF16),
        in_specs=[vm()] * 4,
        out_specs=vm(),
        compiler_params=pltpu.CompilerParams(vmem_limit_bytes=GRANT),
        name="gate",
    )(*near(parts), gate_pre, up_pre, *near(after))


def inputg(acts, d1, d3, width):
    tokens = acts.shape[0] * acts.shape[2]
    return pl.pallas_call(
        input_kernel,
        out_shape=on_chip((2 * tokens, width // 2), BF16),
        in_specs=[vm()] * 3,
        out_specs=vm(),
        compiler_params=pltpu.CompilerParams(vmem_limit_bytes=GRANT),
        name="inputg",
    )(*near(acts, d1, d3))


def near_sum(parts):
    return pl.pallas_call(
        near_kernel,
        out_shape=on_chip(parts.shape[1:], BF16),
        in_specs=[vm()],
        out_specs=vm(),
        compiler_params=pltpu.CompilerParams(vmem_limit_bytes=GRANT),
        name="near_sum",
    )(*near(parts))


def far_sum(parts):
    return pl.pallas_call(
        far_kernel,
        out_shape=jax.ShapeDtypeStruct((parts.shape[1] // 2, 2 * parts.shape[2]), BF16),
        in_specs=[vm()],
        out_specs=vm(),
        compiler_params=pltpu.CompilerParams(vmem_limit_bytes=GRANT),
        name="far_sum",
    )(*near(parts))


def weights(i1, i3, i2, tokens, acts, rows, cols):
    cap = i1.shape[0]
    wide = acts.shape[3]
    count = acts.shape[0] * acts.shape[2]
    o = jax.ShapeDtypeStruct((cap, BLOCK * BLOCK), BF16)
    return pl.pallas_call(
        functools.partial(weight_kernel, rows=rows, cols=cols), out_shape=(o, o, o),
        in_specs=[sm()] * 3 + [vm()] * 2, out_specs=(vm(),) * 3,
        scratch_shapes=[pltpu.VMEM((2 * count, wide), F32), pltpu.VMEM((rows * BLOCK + BLOCK, wide), F32),
            pltpu.VMEM((wide, rows * BLOCK), F32), pltpu.VMEM((cap * BLOCK, 128), F32)],
        compiler_params=pltpu.CompilerParams(vmem_limit_bytes=GRANT), name="weights")(i1, i3, i2, *near(tokens, acts))


def strided(peers, by):
    return [list(range(first, peers, by)) for first in range(by)]


def adjacent(peers, many):
    return [list(range(first, first + many)) for first in range(0, peers, many)]


def gather_tokens(both):
    peers = lax.axis_size("hid")
    skipping = lax.all_gather(both, "hid", axis=0, tiled=True, axis_index_groups=strided(peers, 2))
    return lax.all_gather(skipping, "hid", axis=0, tiled=True, axis_index_groups=adjacent(peers, 2))


def exchange(chunks, groups):
    return lax.all_to_all(chunks, "hid", 0, 0, tiled=True, axis_index_groups=groups)


def scatter_sum(total):
    peers = lax.axis_size("hid")
    width = total.shape[1]
    near = near_sum(exchange(total.reshape(4, -1, width), adjacent(peers, 4)))
    return far_sum(exchange(near.reshape(peers // 4, -1, width), strided(peers, 4)))


def body(
    out_grad,
    inputs,
    gate_pre,
    up_pre,
    w1_values,
    w1_index,
    w3_values,
    w3_index,
    w2_values,
    w2_index,
):
    rows = inputs.shape[1] // BLOCK
    cols = gate_pre.shape[1] // BLOCK
    sections = lax.axis_size("section")
    arrived = lax.ppermute(out_grad, "section", [(i, (i - 1) % sections) for i in range(sections)])
    tokens = gather_tokens(jnp.concatenate([arrived, inputs], axis=0))
    second = densify(w2_index, w2_values, cols, rows)
    first = densify(w1_index, w1_values, rows, cols)
    third = densify(w3_index, w3_values, rows, cols)
    partial_grad = hidden(tokens, second)
    peers = lax.axis_size("wid")
    parts = partial_grad.reshape(peers, partial_grad.shape[0] // peers, partial_grad.shape[1])
    parts = lax.all_to_all(parts, "wid", 0, 0, tiled=True)
    acts = lax.all_to_all(gate(parts, gate_pre, up_pre, third), "wid", 0, 0, tiled=True)
    input_grad = scatter_sum(inputg(acts, first, third, inputs.shape[1]))
    w1_grad, w3_grad, w2_grad = weights(w1_index, w3_index, w2_index, tokens, acts, rows, cols)
    return (input_grad, w1_grad, w3_grad, w2_grad)


def solution(mesh):
    in_specs = (
        P(("section", "hid"), "wid"),
        P(("section", "hid"), "wid"),
        P(("section", "wid"), "hid"),
        P(("section", "wid"), "hid"),
        P(("section", "hid", "wid"), None),
        P(("section", "hid", "wid")),
        P(("section", "hid", "wid"), None),
        P(("section", "hid", "wid")),
        P(("section", "hid", "wid"), None),
        P(("section", "hid", "wid")),
    )
    out_specs = (
        P(("section", "hid"), "wid"),
        P(("section", "hid", "wid"), None),
        P(("section", "hid", "wid"), None),
        P(("section", "hid", "wid"), None),
    )
    return jax.shard_map(body, mesh=mesh, in_specs=in_specs, out_specs=out_specs, check_vma=False)
```

```python
import functools

import jax
import jax.numpy as jnp
from jax import lax
from jax.experimental import pallas as pl
from jax.experimental.pallas import tpu as pltpu
from jax.sharding import PartitionSpec as P

BLOCK = 64
GRANT = 16 << 20
F32, BF16 = jnp.float32, jnp.bfloat16
NT = (((1,), (1,)), ((), ()))
TN = (((0,), (0,)), ((), ()))


def left_half(shape):
    return lax.broadcasted_iota(jnp.int32, shape, len(shape) - 1) < BLOCK


def unpack_blocks(values, spread, cap):
    mask = left_half((cap, 128))
    for pair in range(BLOCK // 2):
        rows = values[:, 128 * pair : 128 * pair + 128].astype(F32)
        turned = pltpu.roll(rows, BLOCK, 1)
        spread[pl.ds(2 * pair, cap, stride=BLOCK), :] = jnp.where(mask, rows, turned)
        spread[pl.ds(2 * pair + 1, cap, stride=BLOCK), :] = jnp.where(mask, turned, rows)


def place_blocks(index, spread, dense, cols, cap):
    lane = lax.broadcasted_iota(jnp.int32, (BLOCK, 128), 1) // BLOCK

    def step(slot, carry):
        number = index[slot]
        row = number // cols
        col = number - row * cols
        block = spread[pl.ds(pl.multiple_of(slot * BLOCK, BLOCK), BLOCK), :].astype(BF16)
        down = pl.ds(pl.multiple_of(row * BLOCK, BLOCK), BLOCK)
        along = pl.ds(pl.multiple_of(col // 2 * 128, 128), 128)
        old = dense[down, along]
        dense[down, along] = jnp.where(lane == col % 2, block, old)
        return carry

    lax.fori_loop(0, cap, step, 0, unroll=4)


def dense_kernel(index, values, dense, spread, *, cols):
    cap = values.shape[0]
    dense[...] = jnp.zeros_like(dense)
    unpack_blocks(values, spread, cap)
    place_blocks(index, spread, dense, cols, cap)


def take_blocks(index, dense, picked, cols, cap):
    def step(slot, carry):
        number = index[slot]
        row = number // cols
        col = number - row * cols
        down = pl.ds(pl.multiple_of(row * BLOCK, BLOCK), BLOCK)
        along = pl.ds(pl.multiple_of(col // 2 * 128, 128), 128)
        block = pltpu.roll(dense[down, along], col % 2 * BLOCK, 1)
        picked[pl.ds(pl.multiple_of(slot * BLOCK, BLOCK), BLOCK), :] = block
        return carry

    lax.fori_loop(0, cap, step, 0, unroll=4)


def pack_blocks(picked, out, cap):
    mask = left_half((cap, 128))
    for pair in range(BLOCK // 2):
        upper = picked[pl.ds(2 * pair, cap, stride=BLOCK), :]
        lower = pltpu.roll(picked[pl.ds(2 * pair + 1, cap, stride=BLOCK), :], BLOCK, 1)
        out[:, 128 * pair : 128 * pair + 128] = jnp.where(mask, upper, lower).astype(BF16)


def hidden_kernel(tokens, dense, out):
    prod = lax.dot_general(tokens[...], dense[...], NT, preferred_element_type=F32)
    width = prod.shape[1]
    top = lax.broadcasted_iota(jnp.int32, (8, width), 0) < 4
    half = prod.shape[0] // 2
    for k in range(half // 8):
        even = prod[8 * k : 8 * k + 8]
        odd = prod[half + 8 * k : half + 8 * k + 8]
        out[8 * k : 8 * k + 8, :] = jnp.where(top, even, pltpu.roll(odd, 4, 0))


def gate_kernel(parts, gate, up, after, out):
    del after
    width = gate.shape[1]
    total = parts[0]
    for i in range(1, parts.shape[0]):
        total = total + parts[i]
    hidden = total[:, :width]
    g = gate[...].astype(F32)
    u = up[...].astype(F32)
    sigma = 1.0 / (1.0 + jnp.exp(-g))
    gate_grad = (hidden * u * sigma * (1.0 + g * (1.0 - sigma))).astype(BF16)
    up_grad = (hidden * g * sigma).astype(BF16)
    activ = (g * sigma * u).astype(BF16)
    out[...] = jnp.zeros_like(out)
    for peer in range(out.shape[0]):
        out[peer, 0, :, :width] = gate_grad
        out[peer, 1, :, :width] = up_grad
        out[peer, 2, :, :width] = activ


def all_rows(acts, which):
    picked = acts[:, which]
    return picked.reshape(picked.shape[0] * picked.shape[1], picked.shape[2])


def input_kernel(parity, acts, d1, d3, kept, sent):
    half = kept.shape[1]
    rows = 2 * half
    prod = lax.dot_general(all_rows(acts, 0), d1[:rows], NT, preferred_element_type=F32)
    prod = prod + lax.dot_general(all_rows(acts, 1), d3[:rows], NT, preferred_element_type=F32)
    top = lax.broadcasted_iota(jnp.int32, (8, half), 0) < 4
    is_even = parity[0] == 0

    def folded(k):
        left, right = prod[8 * k : 8 * k + 8, :half], prod[8 * k : 8 * k + 8, half:]
        even = jnp.where(top, left, pltpu.roll(right, 4, 0))
        odd = jnp.where(top, pltpu.roll(left, 4, 0), right)
        return jnp.where(is_even, even, odd), jnp.where(is_even, odd, even)

    for k in range(0, kept.shape[0] // 8, 2):
        first, second = folded(k), folded(k + 1)
        kept[8 * k : 8 * k + 16, :] = jnp.concatenate([first[0], second[0]], 0)
        sent[8 * k : 8 * k + 16, :] = jnp.concatenate([first[1], second[1]], 0).astype(BF16)


def near_kernel(kept, got, out):
    out[...] = (kept[...] + got[...].astype(F32)).astype(BF16)


def far_kernel(parts, out):
    total = parts[0].astype(F32)
    for i in range(1, parts.shape[0]):
        total = total + parts[i].astype(F32)
    half = total.shape[1]
    out[:, :half] = total[:4].astype(BF16)
    out[:, half:] = pltpu.roll(total, 4, 0)[:4].astype(BF16)


def weight_kernel(i1, i3, i2, tokens, acts, after, o1, o3, o2, spaced, dense, tall, picked, *, rows, cols):
    del after
    cap = o1.shape[0]
    count, width = acts.shape[0] * acts.shape[2], acts.shape[3]
    top = lax.broadcasted_iota(jnp.int32, (8, width), 0) < 4
    zero = jnp.zeros((8, width), F32)

    def spread_rows(which, upper):
        full = all_rows(acts, which).astype(F32)
        for k in range(count // 8):
            piece = full[8 * k : 8 * k + 8]
            turned = pltpu.roll(piece, 4, 0)
            if upper:
                even, odd = jnp.where(top, piece, zero), jnp.where(top, turned, zero)
            else:
                even, odd = jnp.where(top, zero, turned), jnp.where(top, zero, piece)
            spaced[8 * k : 8 * k + 8, :] = even
            spaced[count + 8 * k : count + 8 * k + 8, :] = odd
        return spaced[...].astype(BF16)

    dense[rows * BLOCK :, :] = jnp.zeros((BLOCK, width), F32)
    for which, index, out in ((0, i1, o1), (1, i3, o3)):
        dense[: rows * BLOCK, :] = lax.dot_general(
            tokens[...], spread_rows(which, False), TN, preferred_element_type=F32)
        take_blocks(index, dense, picked, cols, cap)
        pack_blocks(picked, out, cap)
    tall[...] = lax.dot_general(spread_rows(2, True), tokens[...], TN, preferred_element_type=F32)
    take_blocks(i2, tall, picked, rows, cap)
    pack_blocks(picked, o2, cap)


def vm():
    return pl.BlockSpec(memory_space=pltpu.VMEM)


def near(*arrays):
    return tuple(pltpu.with_memory_space_constraint(a, pltpu.VMEM) for a in arrays)


def on_chip(shape, dtype):
    return pltpu.VMEM(shape, dtype)


def sm():
    return pl.BlockSpec(memory_space=pltpu.SMEM)


def densify(index, values, rows, cols):
    cap = values.shape[0]
    wide = (cols + 1) // 2 * 128
    return pl.pallas_call(
        functools.partial(dense_kernel, cols=cols),
        out_shape=on_chip((rows * BLOCK + BLOCK, wide), BF16),
        in_specs=[sm(), vm()],
        out_specs=vm(),
        scratch_shapes=[pltpu.VMEM((cap * BLOCK, 128), F32)],
        compiler_params=pltpu.CompilerParams(vmem_limit_bytes=GRANT),
        name="densify",
    )(index, values)


def hidden(tokens, d2):
    return pl.pallas_call(
        hidden_kernel,
        out_shape=on_chip((tokens.shape[0] // 2, d2.shape[0]), F32),
        in_specs=[vm()] * 2,
        out_specs=vm(),
        compiler_params=pltpu.CompilerParams(vmem_limit_bytes=GRANT),
        name="hidden",
    )(*near(tokens, d2))


def gate(parts, gate_pre, up_pre, after):
    return pl.pallas_call(
        gate_kernel,
        out_shape=on_chip((parts.shape[0], 3) + parts.shape[1:], BF16),
        in_specs=[vm()] * 4,
        out_specs=vm(),
        compiler_params=pltpu.CompilerParams(vmem_limit_bytes=GRANT),
        name="gate",
    )(*near(parts), gate_pre, up_pre, *near(after))


def inputg(parity, acts, d1, d3, width):
    tokens = acts.shape[0] * acts.shape[2]
    return pl.pallas_call(
        input_kernel,
        out_shape=(on_chip((tokens, width // 2), F32), on_chip((tokens, width // 2), BF16)),
        in_specs=[sm()] + [vm()] * 3,
        out_specs=(vm(), vm()),
        compiler_params=pltpu.CompilerParams(vmem_limit_bytes=GRANT),
        name="inputg",
    )(parity, *near(acts, d1, d3))


def near_sum(kept, got):
    return pl.pallas_call(
        near_kernel,
        out_shape=on_chip(got.shape, BF16),
        in_specs=[vm()] * 2,
        out_specs=vm(),
        compiler_params=pltpu.CompilerParams(vmem_limit_bytes=GRANT),
        name="near_sum",
    )(*near(kept, got))


def far_sum(parts):
    return pl.pallas_call(
        far_kernel,
        out_shape=jax.ShapeDtypeStruct((parts.shape[1] // 2, 2 * parts.shape[2]), BF16),
        in_specs=[vm()],
        out_specs=vm(),
        compiler_params=pltpu.CompilerParams(vmem_limit_bytes=GRANT),
        name="far_sum",
    )(*near(parts))


def weights(i1, i3, i2, tokens, acts, after, rows, cols):
    cap = i1.shape[0]
    wide = acts.shape[3]
    count = acts.shape[0] * acts.shape[2]
    o = jax.ShapeDtypeStruct((cap, BLOCK * BLOCK), BF16)
    return pl.pallas_call(
        functools.partial(weight_kernel, rows=rows, cols=cols), out_shape=(o, o, o),
        in_specs=[sm()] * 3 + [vm()] * 2 + [pl.BlockSpec(memory_space=pl.ANY)], out_specs=(vm(),) * 3,
        scratch_shapes=[pltpu.VMEM((2 * count, wide), F32), pltpu.VMEM((rows * BLOCK + BLOCK, wide), F32),
            pltpu.VMEM((wide, rows * BLOCK), F32), pltpu.VMEM((cap * BLOCK, 128), F32)],
        compiler_params=pltpu.CompilerParams(vmem_limit_bytes=GRANT), name="weights")(i1, i3, i2, *near(tokens, acts), after)


def strided(peers, by):
    return [list(range(first, peers, by)) for first in range(by)]


def adjacent(peers, many):
    return [list(range(first, first + many)) for first in range(0, peers, many)]


def gather_tokens(both):
    peers = lax.axis_size("hid")
    skipping = lax.all_gather(both, "hid", axis=0, tiled=True, axis_index_groups=strided(peers, 2))
    return lax.all_gather(skipping, "hid", axis=0, tiled=True, axis_index_groups=adjacent(peers, 2))


def scatter_sum(kept, sent):
    peers = lax.axis_size("hid")
    got = lax.ppermute(sent, "hid", [(peer, peer ^ 1) for peer in range(peers)])
    total = near_sum(kept, got)
    parts = total.reshape(peers // 2, -1, total.shape[1])
    parts = lax.all_to_all(parts, "hid", 0, 0, tiled=True, axis_index_groups=strided(peers, 2))
    return far_sum(parts), total


def body(
    out_grad,
    inputs,
    gate_pre,
    up_pre,
    w1_values,
    w1_index,
    w3_values,
    w3_index,
    w2_values,
    w2_index,
):
    rows = inputs.shape[1] // BLOCK
    cols = gate_pre.shape[1] // BLOCK
    sections = lax.axis_size("section")
    arrived = lax.ppermute(out_grad, "section", [(i, (i - 1) % sections) for i in range(sections)])
    tokens = gather_tokens(jnp.concatenate([arrived, inputs], axis=0))
    second = densify(w2_index, w2_values, cols, rows)
    first = densify(w1_index, w1_values, rows, cols)
    third = densify(w3_index, w3_values, rows, cols)
    partial_grad = hidden(tokens, second)
    peers = lax.axis_size("wid")
    parts = partial_grad.reshape(peers, partial_grad.shape[0] // peers, partial_grad.shape[1])
    parts = lax.all_to_all(parts, "wid", 0, 0, tiled=True)
    acts = lax.all_to_all(gate(parts, gate_pre, up_pre, third), "wid", 0, 0, tiled=True)
    parity = jnp.reshape(lax.axis_index("hid") & 1, (1,)).astype(jnp.int32)
    kept, sent = inputg(parity, acts, first, third, inputs.shape[1])
    input_grad, total = scatter_sum(kept, sent)
    w1_grad, w3_grad, w2_grad = weights(
        w1_index, w3_index, w2_index, tokens, acts, total, rows, cols
    )
    return (input_grad, w1_grad, w3_grad, w2_grad)


def solution(mesh):
    in_specs = (
        P(("section", "hid"), "wid"),
        P(("section", "hid"), "wid"),
        P(("section", "wid"), "hid"),
        P(("section", "wid"), "hid"),
        P(("section", "hid", "wid"), None),
        P(("section", "hid", "wid")),
        P(("section", "hid", "wid"), None),
        P(("section", "hid", "wid")),
        P(("section", "hid", "wid"), None),
        P(("section", "hid", "wid")),
    )
    out_specs = (
        P(("section", "hid"), "wid"),
        P(("section", "hid", "wid"), None),
        P(("section", "hid", "wid"), None),
        P(("section", "hid", "wid"), None),
    )
    return jax.shard_map(body, mesh=mesh, in_specs=in_specs, out_specs=out_specs, check_vma=False)
```

```python
import functools

import jax
import jax.numpy as jnp
from jax import lax
from jax.experimental import pallas as pl
from jax.experimental.pallas import tpu as pltpu
from jax.sharding import PartitionSpec as P

BLOCK = 64
GRANT = 16 << 20
F32, BF16 = jnp.float32, jnp.bfloat16
NT = (((1,), (1,)), ((), ()))
TN = (((0,), (0,)), ((), ()))


def left_half(shape):
    return lax.broadcasted_iota(jnp.int32, shape, len(shape) - 1) < BLOCK


def unpack_blocks(values, spread, cap):
    mask = left_half((cap, 128))
    for pair in range(BLOCK // 2):
        rows = values[:, 128 * pair : 128 * pair + 128].astype(F32)
        turned = pltpu.roll(rows, BLOCK, 1)
        spread[pl.ds(2 * pair, cap, stride=BLOCK), :] = jnp.where(mask, rows, turned)
        spread[pl.ds(2 * pair + 1, cap, stride=BLOCK), :] = jnp.where(mask, turned, rows)


def place_blocks(index, spread, dense, cols, cap):
    lane = lax.broadcasted_iota(jnp.int32, (BLOCK, 128), 1) // BLOCK

    def step(slot, carry):
        number = index[slot]
        row = number // cols
        col = number - row * cols
        block = spread[pl.ds(pl.multiple_of(slot * BLOCK, BLOCK), BLOCK), :].astype(BF16)
        down = pl.ds(pl.multiple_of(row * BLOCK, BLOCK), BLOCK)
        along = pl.ds(pl.multiple_of(col // 2 * 128, 128), 128)
        old = dense[down, along]
        dense[down, along] = jnp.where(lane == col % 2, block, old)
        return carry

    lax.fori_loop(0, cap, step, 0, unroll=4)


def dense_kernel(index, values, dense, spread, *, cols):
    cap = values.shape[0]
    dense[...] = jnp.zeros_like(dense)
    unpack_blocks(values, spread, cap)
    place_blocks(index, spread, dense, cols, cap)


def take_blocks(index, dense, picked, cols, cap):
    def step(slot, carry):
        number = index[slot]
        row = number // cols
        col = number - row * cols
        down = pl.ds(pl.multiple_of(row * BLOCK, BLOCK), BLOCK)
        along = pl.ds(pl.multiple_of(col // 2 * 128, 128), 128)
        block = pltpu.roll(dense[down, along], col % 2 * BLOCK, 1)
        picked[pl.ds(pl.multiple_of(slot * BLOCK, BLOCK), BLOCK), :] = block
        return carry

    lax.fori_loop(0, cap, step, 0, unroll=4)


def pack_blocks(picked, out, cap):
    mask = left_half((cap, 128))
    for pair in range(BLOCK // 2):
        upper = picked[pl.ds(2 * pair, cap, stride=BLOCK), :]
        lower = pltpu.roll(picked[pl.ds(2 * pair + 1, cap, stride=BLOCK), :], BLOCK, 1)
        out[:, 128 * pair : 128 * pair + 128] = jnp.where(mask, upper, lower).astype(BF16)


def hidden_kernel(tokens, dense, out):
    prod = lax.dot_general(tokens[...], dense[...], NT, preferred_element_type=F32)
    width = prod.shape[1]
    top = lax.broadcasted_iota(jnp.int32, (8, width), 0) < 4
    half = prod.shape[0] // 2
    for k in range(half // 8):
        even = prod[8 * k : 8 * k + 8]
        odd = prod[half + 8 * k : half + 8 * k + 8]
        out[8 * k : 8 * k + 8, :] = jnp.where(top, even, pltpu.roll(odd, 4, 0))


def gate_kernel(parts, gate, up, after, out):
    del after
    width = gate.shape[1]
    total = parts[0]
    for i in range(1, parts.shape[0]):
        total = total + parts[i]
    hidden = total[:, :width]
    g = gate[...].astype(F32)
    u = up[...].astype(F32)
    sigma = 1.0 / (1.0 + jnp.exp(-g))
    gate_grad = (hidden * u * sigma * (1.0 + g * (1.0 - sigma))).astype(BF16)
    up_grad = (hidden * g * sigma).astype(BF16)
    activ = (g * sigma * u).astype(BF16)
    out[...] = jnp.zeros_like(out)
    for peer in range(out.shape[0]):
        out[peer, 0, :, :width] = gate_grad
        out[peer, 1, :, :width] = up_grad
        out[peer, 2, :, :width] = activ


def all_rows(acts, which):
    picked = acts[:, which]
    return picked.reshape(picked.shape[0] * picked.shape[1], picked.shape[2])


def input_kernel(parity, acts, d1, d3, kept, sent):
    half = kept.shape[1]
    rows = 2 * half
    prod = lax.dot_general(all_rows(acts, 0), d1[:rows], NT, preferred_element_type=F32)
    prod = prod + lax.dot_general(all_rows(acts, 1), d3[:rows], NT, preferred_element_type=F32)
    top = lax.broadcasted_iota(jnp.int32, (8, half), 0) < 4
    is_even = parity[0] == 0

    def folded(k):
        left, right = prod[8 * k : 8 * k + 8, :half], prod[8 * k : 8 * k + 8, half:]
        even = jnp.where(top, left, pltpu.roll(right, 4, 0))
        odd = jnp.where(top, pltpu.roll(left, 4, 0), right)
        return jnp.where(is_even, even, odd), jnp.where(is_even, odd, even)

    for k in range(0, kept.shape[0] // 8, 2):
        first, second = folded(k), folded(k + 1)
        kept[8 * k : 8 * k + 16, :] = jnp.concatenate([first[0], second[0]], 0)
        sent[8 * k : 8 * k + 16, :] = jnp.concatenate([first[1], second[1]], 0).astype(BF16)


def near_kernel(kept, got, out):
    out[...] = (kept[...] + got[...].astype(F32)).astype(BF16)


def far_kernel(parts, out):
    total = parts[0].astype(F32)
    for i in range(1, parts.shape[0]):
        total = total + parts[i].astype(F32)
    half = total.shape[1]
    out[:, :half] = total[:4].astype(BF16)
    out[:, half:] = pltpu.roll(total, 4, 0)[:4].astype(BF16)


def weight_kernel(i1, i3, i2, tokens, acts, after, o1, o3, o2, spaced, dense, tall, picked, *, rows, cols):
    del after
    cap = o1.shape[0]
    count, width = acts.shape[0] * acts.shape[2], acts.shape[3]
    top = lax.broadcasted_iota(jnp.int32, (8, width), 0) < 4
    zero = jnp.zeros((8, width), F32)

    def spread_rows(which, upper):
        full = all_rows(acts, which).astype(F32)
        for k in range(count // 8):
            piece = full[8 * k : 8 * k + 8]
            turned = pltpu.roll(piece, 4, 0)
            if upper:
                even, odd = jnp.where(top, piece, zero), jnp.where(top, turned, zero)
            else:
                even, odd = jnp.where(top, zero, turned), jnp.where(top, zero, piece)
            spaced[8 * k : 8 * k + 8, :] = even
            spaced[count + 8 * k : count + 8 * k + 8, :] = odd
        return spaced[...].astype(BF16)

    dense[rows * BLOCK :, :] = jnp.zeros((BLOCK, width), F32)
    for which, index, out in ((0, i1, o1), (1, i3, o3)):
        dense[: rows * BLOCK, :] = lax.dot_general(
            tokens[...], spread_rows(which, False), TN, preferred_element_type=F32)
        take_blocks(index, dense, picked, cols, cap)
        pack_blocks(picked, out, cap)
    tall[...] = lax.dot_general(spread_rows(2, True), tokens[...], TN, preferred_element_type=F32)
    take_blocks(i2, tall, picked, rows, cap)
    pack_blocks(picked, o2, cap)


def vm():
    return pl.BlockSpec(memory_space=pltpu.VMEM)


def near(*arrays):
    return tuple(pltpu.with_memory_space_constraint(a, pltpu.VMEM) for a in arrays)


def far_off(array):
    return pltpu.with_memory_space_constraint(array, pltpu.HBM)


def on_chip(shape, dtype):
    return pltpu.VMEM(shape, dtype)


def sm():
    return pl.BlockSpec(memory_space=pltpu.SMEM)


def densify(index, values, rows, cols):
    cap = values.shape[0]
    wide = (cols + 1) // 2 * 128
    return pl.pallas_call(
        functools.partial(dense_kernel, cols=cols),
        out_shape=on_chip((rows * BLOCK + BLOCK, wide), BF16),
        in_specs=[sm(), vm()],
        out_specs=vm(),
        scratch_shapes=[pltpu.VMEM((cap * BLOCK, 128), F32)],
        compiler_params=pltpu.CompilerParams(vmem_limit_bytes=GRANT),
        name="densify",
    )(index, values)


def hidden(tokens, d2):
    return pl.pallas_call(
        hidden_kernel,
        out_shape=on_chip((tokens.shape[0] // 2, d2.shape[0]), F32),
        in_specs=[vm()] * 2,
        out_specs=vm(),
        compiler_params=pltpu.CompilerParams(vmem_limit_bytes=GRANT),
        name="hidden",
    )(*near(tokens, d2))


def gate(parts, gate_pre, up_pre, after):
    return pl.pallas_call(
        gate_kernel,
        out_shape=on_chip((parts.shape[0], 3) + parts.shape[1:], BF16),
        in_specs=[vm()] * 4,
        out_specs=vm(),
        compiler_params=pltpu.CompilerParams(vmem_limit_bytes=GRANT),
        name="gate",
    )(*near(parts), gate_pre, up_pre, *near(after))


def inputg(parity, acts, d1, d3, width):
    tokens = acts.shape[0] * acts.shape[2]
    return pl.pallas_call(
        input_kernel,
        out_shape=(on_chip((tokens, width // 2), F32), on_chip((tokens, width // 2), BF16)),
        in_specs=[sm()] + [vm()] * 3,
        out_specs=(vm(), vm()),
        compiler_params=pltpu.CompilerParams(vmem_limit_bytes=GRANT),
        name="inputg",
    )(parity, *near(acts, d1, d3))


def near_sum(kept, got):
    return pl.pallas_call(
        near_kernel,
        out_shape=on_chip(got.shape, BF16),
        in_specs=[vm()] * 2,
        out_specs=vm(),
        compiler_params=pltpu.CompilerParams(vmem_limit_bytes=GRANT),
        name="near_sum",
    )(*near(kept, got))


def far_sum(parts):
    return pl.pallas_call(
        far_kernel,
        out_shape=jax.ShapeDtypeStruct((parts.shape[1] // 2, 2 * parts.shape[2]), BF16),
        in_specs=[vm()],
        out_specs=vm(),
        compiler_params=pltpu.CompilerParams(vmem_limit_bytes=GRANT),
        name="far_sum",
    )(*near(parts))


def weights(i1, i3, i2, tokens, acts, after, rows, cols):
    cap = i1.shape[0]
    wide = acts.shape[3]
    count = acts.shape[0] * acts.shape[2]
    o = jax.ShapeDtypeStruct((cap, BLOCK * BLOCK), BF16)
    return pl.pallas_call(
        functools.partial(weight_kernel, rows=rows, cols=cols), out_shape=(o, o, o),
        in_specs=[sm()] * 3 + [vm()] * 2 + [pl.BlockSpec(memory_space=pl.ANY)], out_specs=(vm(),) * 3,
        scratch_shapes=[pltpu.VMEM((2 * count, wide), F32), pltpu.VMEM((rows * BLOCK + BLOCK, wide), F32),
            pltpu.VMEM((wide, rows * BLOCK), F32), pltpu.VMEM((cap * BLOCK, 128), F32)],
        compiler_params=pltpu.CompilerParams(vmem_limit_bytes=GRANT), name="weights")(i1, i3, i2, *near(tokens, acts), after)


def strided(peers, by):
    return [list(range(first, peers, by)) for first in range(by)]


def adjacent(peers, many):
    return [list(range(first, first + many)) for first in range(0, peers, many)]


def gather_tokens(both):
    peers = lax.axis_size("hid")
    skipping = lax.all_gather(both, "hid", axis=0, tiled=True, axis_index_groups=strided(peers, 2))
    return lax.all_gather(skipping, "hid", axis=0, tiled=True, axis_index_groups=adjacent(peers, 2))


def scatter_sum(kept, sent):
    peers = lax.axis_size("hid")
    got = lax.ppermute(sent, "hid", [(peer, peer ^ 1) for peer in range(peers)])
    total = near_sum(kept, got)
    parts = total.reshape(peers // 2, -1, total.shape[1])
    parts = lax.all_to_all(parts, "hid", 0, 0, tiled=True, axis_index_groups=strided(peers, 2))
    return far_sum(parts), total


def body(
    out_grad,
    inputs,
    gate_pre,
    up_pre,
    w1_values,
    w1_index,
    w3_values,
    w3_index,
    w2_values,
    w2_index,
):
    rows = inputs.shape[1] // BLOCK
    cols = gate_pre.shape[1] // BLOCK
    sections = lax.axis_size("section")
    arrived = lax.ppermute(out_grad, "section", [(i, (i - 1) % sections) for i in range(sections)])
    tokens = gather_tokens(jnp.concatenate([arrived, inputs], axis=0))
    second = densify(far_off(w2_index), far_off(w2_values), cols, rows)
    first = densify(w1_index, w1_values, rows, cols)
    third = densify(w3_index, w3_values, rows, cols)
    partial_grad = hidden(tokens, second)
    peers = lax.axis_size("wid")
    parts = partial_grad.reshape(peers, partial_grad.shape[0] // peers, partial_grad.shape[1])
    parts = lax.all_to_all(parts, "wid", 0, 0, tiled=True)
    acts = lax.all_to_all(gate(parts, gate_pre, up_pre, third), "wid", 0, 0, tiled=True)
    parity = jnp.reshape(lax.axis_index("hid") & 1, (1,)).astype(jnp.int32)
    kept, sent = inputg(parity, acts, first, third, inputs.shape[1])
    input_grad, total = scatter_sum(kept, sent)
    w1_grad, w3_grad, w2_grad = weights(
        w1_index, w3_index, w2_index, tokens, acts, total, rows, cols
    )
    return (input_grad, w1_grad, w3_grad, w2_grad)


def solution(mesh):
    in_specs = (
        P(("section", "hid"), "wid"),
        P(("section", "hid"), "wid"),
        P(("section", "wid"), "hid"),
        P(("section", "wid"), "hid"),
        P(("section", "hid", "wid"), None),
        P(("section", "hid", "wid")),
        P(("section", "hid", "wid"), None),
        P(("section", "hid", "wid")),
        P(("section", "hid", "wid"), None),
        P(("section", "hid", "wid")),
    )
    out_specs = (
        P(("section", "hid"), "wid"),
        P(("section", "hid", "wid"), None),
        P(("section", "hid", "wid"), None),
        P(("section", "hid", "wid"), None),
    )
    return jax.shard_map(body, mesh=mesh, in_specs=in_specs, out_specs=out_specs, check_vma=False)
```
